32 devices in a mesh: tp: 4 (over y, x), grp: 8 (over z, core).
Axes of the slice: x: 2, y: 2, z: 4, core: 2. Of those that a mesh axis runs over, the one named last changes fastest.
Arguments:
- embeds: bfloat16 [2, 32, 8192], P(None, 'grp'), may hold values from -6 to 6
- ssm_state: bfloat16 [2, 32, 128, 64, 128], P(None, 'grp', 'tp'), may hold values from -2 to 2
- conv_state: bfloat16 [2, 32, 3, 8192], P(None, 'grp', None, 'tp'), may hold values from -6 to 6
- norm_gain: float32 [2, 8192], replicated, may hold values from 0.25 to 1.75
- in_weight: bfloat16 [2, 8192, 2, 8192], P(None, 'grp', None, 'tp'), may hold values from -0.0625 to 0.0625
- group_weight: bfloat16 [2, 8192, 384], P(None, 'grp'), may hold values from -0.03125 to 0.03125
- dt_bias: float32 [2, 128], P(None, 'tp'), may hold values from -2 to 1
- a_log: float32 [2, 128], P(None, 'tp'), may hold values from -1.5 to 1.5
- skip_gain: float32 [2, 128], P(None, 'tp'), may hold values from 0.5 to 1.5
- conv_weight: float32 [2, 4, 8192], P(None, None, 'tp'), may hold values from -3 to 3
- conv_bias: float32 [2, 8192], P(None, 'tp'), may hold values from -2 to 2
- out_weight: bfloat16 [2, 8192, 8192], P(None, 'tp', 'grp'), may hold values from -0.0625 to 0.0625
- leave_row: int32 [8], P('grp'), may hold values from 0 to 3
- arrive_from: int32 [8], P('grp'), may hold values from 0 to 7, as said below
Outputs:
- out_hidden: bfloat16 [2, 32, 8192], P(None, 'grp', 'tp')
The draws below stay inside these ranges and needn't reach their ends.
Inputs may be any that keep to these rules, and one draw needn't show every extreme that they name: Every group appears exactly once in arrive_from: each group's leaving row fills exactly one freed slot.
All inputs are finite; a program needn't handle non-finite values.
Results may differ from the reference program's by a relative error of at most 0.02.
Values may be sent and summed in bfloat16 or wider, within the bound.
A program may use at most 128 MiB of HBM per device.

```python
import jax
import jax.numpy as jnp
from jax import lax

D = 8192
HEAD_DIM = 64
CONV = 4
INNER = 8192
STATE = 128
LAYERS = 2
STEPS = 2
ROW_DEV = 4
HEADS = 128
GROUPS = 8
ROWS = 32


def place_value(perm, position, wanted):
    where_now = jnp.argmax(perm == wanted).astype(jnp.int32)
    previous = perm[position]
    perm = perm.at[where_now].set(previous)
    return perm.at[position].set(wanted)


def draw_arrive_from(key, part):
    perm = jax.random.permutation(jax.random.fold_in(key, 11), GROUPS).astype(jnp.int32)
    first = jax.random.randint(jax.random.fold_in(key, 12), (), 0, GROUPS).astype(jnp.int32)
    half_away = ((first + GROUPS // 2) % GROUPS).astype(jnp.int32)
    perm = place_value(perm, first, half_away)
    beside = ((first + 1) % GROUPS).astype(jnp.int32)
    perm = place_value(perm, beside, first)
    return perm.astype(jnp.int32)


def with_ends(entries, key, least, largest):
    spot = [jax.random.randint(jax.random.fold_in(key, axis), (), 0, length) for axis, length in enumerate(entries.shape)]
    longest = entries.shape.index(max(entries.shape))
    neighbour = spot[:longest] + [(spot[longest] + 1) % entries.shape[longest]] + spot[longest + 1:]
    return entries.at[tuple(spot)].set(least).at[tuple(neighbour)].set(largest)


def block_scale(key, extent, cuts, smallest, top_value):
    def one(dim, shards_of):
        steps = jax.random.uniform(jax.random.fold_in(jax.random.fold_in(key, 6), dim), (shards_of,), jnp.float32, smallest / len(cuts), top_value / len(cuts))
        return jnp.repeat(jnp.exp(steps), extent[dim] // shards_of).reshape((-1,) + (1,) * (len(extent) - dim - 1))

    level = one(*cuts[0])
    for cut in cuts[1:]:
        level = level * one(*cut)
    return level


def normal_values(stream_key, dims, scale, reach, pieces=(), held_as=jnp.bfloat16):
    array = jax.random.normal(stream_key, dims, jnp.float32) * scale
    if len(pieces) > 0:
        array = block_scale(stream_key, dims, pieces, -0.22, 0.18) * array
    return jnp.clip(array, min=-reach, max=reach).astype(held_as)


def setup_inputs(seed: int = 0) -> dict:
    arg_keys = jax.random.split(jax.random.key(seed), 15)
    embeds = normal_values(arg_keys[0], (STEPS, ROWS, D), 1.0, 6.0, ((1, 8),))
    ssm_state = normal_values(arg_keys[1], (LAYERS, ROWS, HEADS, HEAD_DIM, STATE), 0.3, 2.0, ((1, 8), (2, 4)))
    conv_state = normal_values(arg_keys[2], (LAYERS, ROWS, CONV - 1, INNER), 1.0, 6.0, ((1, 8), (3, 4)))
    norm_gain = jnp.clip(1.0 + 0.15 * jax.random.normal(arg_keys[3], (LAYERS, D), jnp.float32), 0.25, 1.75)
    in_weight = normal_values(arg_keys[4], (LAYERS, D, 2, INNER), D ** -0.5, 0.0625, ((1, 8), (3, 4)))
    group_weight = normal_values(arg_keys[5], (LAYERS, D, 2 * STATE + HEADS), (4 * D) ** -0.5, 0.03125, ((1, 8),))
    dt_bias = jnp.clip(-2.0 + 3.0 * jax.random.uniform(arg_keys[6], (LAYERS, HEADS), jnp.float32) ** block_scale(arg_keys[6], (LAYERS, HEADS), ((1, 4),), -0.2, 0.2), -2.0, 1.0)
    a_log = jnp.clip(jax.random.uniform(arg_keys[7], (LAYERS, HEADS), jnp.float32, -1.5, 1.5) * block_scale(arg_keys[7], (LAYERS, HEADS), ((1, 4),), -0.4, 0.0), -1.5, 1.5)
    skip_gain = jnp.clip(0.5 + 1.0 * jax.random.uniform(arg_keys[8], (LAYERS, HEADS), jnp.float32) ** block_scale(arg_keys[8], (LAYERS, HEADS), ((1, 4),), -0.2, 0.2), 0.5, 1.5)
    conv_weight = normal_values(arg_keys[9], (LAYERS, CONV, INNER), 0.5, 3.0, ((2, 4),), jnp.float32)
    conv_bias = normal_values(arg_keys[10], (LAYERS, INNER), 0.3, 2.0, ((1, 4),), jnp.float32)
    out_weight = normal_values(arg_keys[11], (LAYERS, INNER, D), INNER ** -0.5, 0.0625, ((1, 4), (2, 8)))
    leave_row = with_ends(jax.random.randint(arg_keys[12], (GROUPS,), 0, ROW_DEV), jax.random.fold_in(arg_keys[12], 1), 0, ROW_DEV - 1).astype(jnp.int32)
    arrive_from = draw_arrive_from(jax.random.fold_in(arg_keys[14], 71), 0)
    return {"embeds": embeds, "ssm_state": ssm_state, "conv_state": conv_state, "norm_gain": norm_gain, "in_weight": in_weight, "group_weight": group_weight, "dt_bias": dt_bias, "a_log": a_log, "skip_gain": skip_gain, "conv_weight": conv_weight, "conv_bias": conv_bias, "out_weight": out_weight, "leave_row": leave_row, "arrive_from": arrive_from}


def mamba_layer(hidden, state, conv, gain, w_in, w_group, bias_dt, log_rate, skip, taps, conv_off, w_out):
    rows = hidden.shape[0]
    hf = hidden.astype(jnp.float32)
    normed = (hf * lax.rsqrt(lax.optimization_barrier(jnp.mean(hf * hf, axis=-1, keepdims=True)) + 1e-05) * gain).astype(jnp.bfloat16)
    proj = jnp.dot(normed, w_in.reshape(D, 2 * INNER), preferred_element_type=jnp.float32)
    x_part = proj[:, :INNER].astype(jnp.bfloat16)
    z_part = proj[:, INNER:]
    mix = jnp.dot(normed, w_group, preferred_element_type=jnp.float32)
    b_mat = mix[:, :STATE]
    c_mat = mix[:, STATE:2 * STATE]
    dt_raw = mix[:, 2 * STATE:]
    conv_sum = x_part.astype(jnp.float32) * taps[CONV - 1] + conv_off
    for k in range(CONV - 1):
        conv_sum = conv_sum + conv[:, k].astype(jnp.float32) * taps[k]
    xc = jax.nn.silu(conv_sum)
    new_conv = jnp.concatenate([conv[:, 1:], x_part[:, None, :]], axis=1)
    step_size = jax.nn.softplus(dt_raw + bias_dt)
    decay = jnp.exp(-step_size * jnp.exp(log_rate))
    xh = xc.reshape(rows, HEADS, HEAD_DIM)
    fresh = state.astype(jnp.float32) * decay[:, :, None, None] + (step_size[:, :, None] * xh)[..., None] * b_mat[:, None, None, :]
    out_y = lax.optimization_barrier(jnp.sum(fresh * c_mat[:, None, None, :], axis=-1)) + skip[None, :, None] * xh
    gated = (out_y.reshape(rows, INNER) * jax.nn.silu(z_part)).astype(jnp.bfloat16)
    delta = jnp.dot(gated, w_out, preferred_element_type=jnp.float32).astype(jnp.bfloat16)
    hidden = (hf + delta.astype(jnp.float32)).astype(jnp.bfloat16)
    return (hidden, fresh.astype(jnp.bfloat16), new_conv)

def reference(embeds, ssm_state, conv_state, norm_gain, in_weight, group_weight, dt_bias, a_log, skip_gain, conv_weight, conv_bias, out_weight, leave_row, arrive_from):
    states = [ssm_state[i] for i in range(LAYERS)]
    convs = [conv_state[i] for i in range(LAYERS)]
    groups_idx = jnp.arange(GROUPS, dtype=jnp.int32)
    target = (groups_idx * ROW_DEV + leave_row).astype(jnp.int32)
    source = (arrive_from * ROW_DEV + leave_row[arrive_from]).astype(jnp.int32)
    results = []
    for section in range(STEPS):
        if section > 0:
            for i in range(LAYERS):
                states[i] = states[i].at[target].set(states[i][source])
                convs[i] = convs[i].at[target].set(convs[i][source])
        hidden = embeds[section]
        for i in range(LAYERS):
            hidden, states[i], convs[i] = mamba_layer(hidden, states[i], convs[i], norm_gain[i], in_weight[i], group_weight[i], dt_bias[i], a_log[i], skip_gain[i], conv_weight[i], conv_bias[i], out_weight[i])
        results.append(hidden)
    return jnp.stack(results)
```

```python
import functools

import jax
import jax.numpy as jnp
from jax import lax
from jax.experimental import pallas as pl
from jax.experimental.pallas import tpu as pltpu
from jax.sharding import PartitionSpec as P

F32 = jnp.float32
BF = jnp.bfloat16
LANES = 128


def iota(shape, dim):
    return lax.broadcasted_iota(jnp.int32, shape, dim)


def mm(a, b):
    return jnp.dot(a, b, preferred_element_type=F32)


def silu(v):
    return v / (1.0 + jnp.exp(-v))


def remote(src, dst, send_sem, recv_sem, axis, peer):
    return pltpu.make_async_remote_copy(
        src_ref=src,
        dst_ref=dst,
        send_sem=send_sem,
        recv_sem=recv_sem,
        device_id={axis: peer},
        device_id_type=pl.DeviceIdType.MESH,
    )


def kernel(
    groups, parts, heads_dev, head_dim, chunk_in, chunk_out,
    emb, conv, gain, head, taps, cbias, info, state, w_in, w_grp, w_out,
    out,
    win_v, wg_v, wout_v, st_v,
    emb_r, info_r, e32, info32, pre, sel, lhs, hxs,
    m_send, m_recv, a_send, a_recv, b_send, b_recv, c_send, c_recv, o_send, o_recv,
    hl, y8, xz, gat, o32, keep_d, keep_u, keep_x, keep_b,
    load_sem, es_sem, er_sem, is_sem, ir_sem, ms_sem, mr_sem, as_sem, ar_sem,
    bs_sem, br_sem, cs_sem, cr_sem, os_sem, or_sem,
):
    g = lax.axis_index("grp")
    t = lax.axis_index("tp")
    steps, row_dev, width = emb.shape
    layers = gain.shape[0]
    block = width // groups
    rows = groups * row_dev
    pair = 2 * row_dev
    channels = taps.shape[2]
    taps_count = taps.shape[1]
    state_dim = st_v.shape[3]
    mix_width = wg_v.shape[2]
    n_in = channels // chunk_in
    n_out = block // chunk_out
    share = groups // parts

    loads = []
    for l in range(layers):
        for i, (src, dst) in enumerate(
            ((w_grp, wg_v), (w_in, win_v), (state, st_v), (w_out, wout_v))
        ):
            cp = pltpu.make_async_copy(src.at[l], dst.at[l], load_sem.at[l, i])
            cp.start()
            loads.append(cp)

    barrier = pltpu.get_barrier_semaphore()
    for d in range(1, groups):
        pl.semaphore_signal(
            barrier, inc=1, device_id={"grp": lax.rem(g + d, groups)},
            device_id_type=pl.DeviceIdType.MESH,
        )
    for d in range(1, parts):
        pl.semaphore_signal(
            barrier, inc=1, device_id={"tp": lax.rem(t + d, parts)},
            device_id_type=pl.DeviceIdType.MESH,
        )
    pl.semaphore_wait(barrier, groups - 1 + parts - 1)

    def columns(who):
        return pl.ds(pl.multiple_of(who * block, block), block)

    first_sends = []
    for d in range(1, groups):
        peer = lax.rem(g + d, groups)
        cp = remote(emb.at[:, :, columns(peer)], emb_r.at[g], es_sem.at[d], er_sem.at[g], "grp", peer)
        cp.start()
        first_sends.append(cp)
        cp = remote(info, info_r.at[g], is_sem.at[d], ir_sem.at[g], "grp", peer)
        cp.start()
        first_sends.append(cp)
    emb_r[g] = emb[:, :, columns(g)]
    info_r[g] = info[...]

    for s in range(steps):
        for l in range(layers):
            total = jnp.zeros((row_dev, channels), F32)
            for k in range(taps_count - 1):
                if s + k <= taps_count - 2:
                    total = total + conv[l, s + k].astype(F32) * taps[l, k : k + 1, :]
            pre[s, l] = total + cbias[l : l + 1, :]
    n_heads = sel.shape[0]
    sel[...] = (
        iota((n_heads, channels), 0) == t * heads_dev + iota((n_heads, channels), 1) // head_dim
    ).astype(F32).astype(BF)
    dup_row = iota((2 * rows, rows), 0)
    dup = (
        iota((2 * rows, rows), 1) == (dup_row // pair) * row_dev + lax.rem(dup_row, row_dev)
    ).astype(F32).astype(BF)
    und_col = iota((rows, 2 * rows), 1)
    und_row = iota((rows, 2 * rows), 0)
    undup = (
        und_col == (und_row // row_dev) * pair + lax.rem(und_row, row_dev)
    ).astype(F32).astype(BF)
    spread = (
        iota((LANES, 2 * LANES), 1) // 2 == iota((LANES, 2 * LANES), 0)
    ).astype(F32).astype(BF)
    own_half = lax.rem(iota((2 * rows, 2 * LANES), 1), 2) == lax.rem(
        iota((2 * rows, 2 * LANES), 0) // row_dev, 2
    )

    for d in range(1, groups):
        src = lax.rem(g + groups - d, groups)
        remote(emb.at[:, :, columns(src)], emb_r.at[src], es_sem.at[d], er_sem.at[src], "grp", src).wait_recv()
        remote(info, info_r.at[src], is_sem.at[d], ir_sem.at[src], "grp", src).wait_recv()
    for i in range(groups):
        for s in range(steps):
            e32[s, i * row_dev : (i + 1) * row_dev, :] = emb_r[i, s].astype(F32)
        for q in range(2):
            info32[q, i * row_dev : (i + 1) * row_dev, :] = info_r[i, q]

    row_i = iota((rows, LANES), 0)
    col_i = iota((rows, LANES), 1)
    on_diag = row_i == col_i
    leave_of_row = info32[0]
    from_of_row = info32[1]
    leave_of_col = jnp.sum(jnp.where(on_diag, leave_of_row, 0.0), axis=0, keepdims=True)
    from_of_col = jnp.sum(jnp.where(on_diag, from_of_row, 0.0), axis=0, keepdims=True)
    slot_row = lax.rem(row_i, row_dev).astype(F32)
    slot_col = lax.rem(col_i, row_dev).astype(F32)
    group_row = (row_i // row_dev).astype(F32)
    group_col = (col_i // row_dev).astype(F32)
    diag = jnp.where(on_diag, 1.0, 0.0)
    hit = jnp.where(group_col == from_of_row, 1.0, 0.0) * jnp.where(slot_col == leave_of_col, 1.0, 0.0)
    to_slot = jnp.where(slot_row == leave_of_row, hit, diag)[:, :rows].astype(BF)
    hit_t = jnp.where(group_row == from_of_col, 1.0, 0.0) * jnp.where(slot_row == leave_of_row, 1.0, 0.0)
    to_home = jnp.where(slot_col == leave_of_col, hit_t, diag)[:, :rows].astype(BF)

    for cp in first_sends:
        cp.wait_send()

    out_sends = []
    for s in range(steps):
        start = e32[s].astype(BF)
        for _ in range(s):
            start = mm(to_home, start).astype(BF)
        hxs[...] = mm(dup, start)
        for l in range(layers):
            k = s * layers + l
            sends = []
            hx = hxs[...]
            gained = (hx * gain[l : l + 1, columns(g)]).astype(BF)
            if s == 0:
                loads[4 * l].wait()
            mix = mm(gained, wg_v[l])
            square = jnp.broadcast_to(jnp.sum(hx * hx, axis=1, keepdims=True), (2 * rows, LANES))
            for i in range(groups):
                m_send[i, :, :mix_width] = mix[i * pair : i * pair + row_dev]
                m_send[i, :, mix_width:] = square[i * pair : i * pair + row_dev]
            for d in range(1, groups):
                peer = lax.rem(g + d, groups)
                cp = remote(m_send.at[peer], m_recv.at[k, g], ms_sem.at[d], mr_sem.at[k, g], "grp", peer)
                cp.start()
                sends.append(cp)
            m_recv[k, g] = m_send[g]
            for j in range(block // LANES):
                wide = mm(gained[:, j * LANES : (j + 1) * LANES], spread)
                lhs[:, 2 * j * LANES : 2 * (j + 1) * LANES] = jnp.where(own_half, wide, 0.0).astype(BF)
            if s == 0:
                loads[4 * l + 1].wait()
            for c in range(n_in):
                acc = mm(lhs[...], win_v[l, :, c * chunk_in : (c + 1) * chunk_in])
                for i in range(groups):
                    a_send[c, i] = acc[i * pair : (i + 1) * pair].astype(BF)
                for d in range(1, groups):
                    peer = lax.rem(g + d, groups)
                    cp = remote(
                        a_send.at[c, peer], a_recv.at[k, c, g], as_sem.at[c, d], ar_sem.at[k, c, g], "grp", peer
                    )
                    cp.start()
                    sends.append(cp)
                a_recv[k, c, g] = a_send[c, g]

            for d in range(1, groups):
                src = lax.rem(g + groups - d, groups)
                remote(m_send.at[src], m_recv.at[k, src], ms_sem.at[d], mr_sem.at[k, src], "grp", src).wait_recv()
            msum = m_recv[k, 0]
            for i in range(1, groups):
                msum = msum + m_recv[k, i]
            scale = lax.rsqrt(msum[:, mix_width : mix_width + 1] / width + 1e-05)
            b_mat = msum[:, :state_dim] * scale
            c_mat = msum[:, state_dim : 2 * state_dim] * scale
            dt_all = msum[:, 2 * state_dim : mix_width] * scale
            keep_b[l, s] = b_mat
            dt_hi = dt_all.astype(BF)
            dt_lo = (dt_all - dt_hi.astype(F32)).astype(BF)
            dt_ch = mm(dt_hi, sel[...]) + mm(dt_lo, sel[...])
            pre_dt = dt_ch + head[0, l : l + 1, :]
            step_size = jnp.maximum(pre_dt, 0.0) + jnp.log1p(jnp.exp(-jnp.abs(pre_dt)))
            keep_d[l, s] = jnp.exp(-step_size * jnp.exp(head[1, l : l + 1, :]))
            c_hi = c_mat.astype(BF).astype(F32)
            hl[0:row_dev, :] = c_hi
            hl[row_dev:pair, :] = c_mat - c_hi
            c_both = hl[...].astype(BF)
            if s == 0:
                loads[4 * l + 2].wait()
            slot8 = lax.rem(iota((pair, channels), 0), row_dev)
            total = jnp.zeros((pair, channels), F32)
            for r in range(row_dev):
                got = lax.dot_general(
                    c_both, st_v[l, r], (((1,), (1,)), ((), ())), preferred_element_type=F32
                )
                total = jnp.where(slot8 == r, got, total)
            y8[...] = total
            acc_y = y8[0:row_dev, :] + y8[row_dev:pair, :]

            for c in range(n_in):
                for d in range(1, groups):
                    src = lax.rem(g + groups - d, groups)
                    remote(
                        a_send.at[c, src], a_recv.at[k, c, src], as_sem.at[c, d], ar_sem.at[k, c, src], "grp", src
                    ).wait_recv()
                asum = a_recv[k, c, 0].astype(F32)
                for i in range(1, groups):
                    asum = asum + a_recv[k, c, i].astype(F32)
                xz[:, c * chunk_in : (c + 1) * chunk_in] = asum
            x = (xz[0:row_dev, :] * scale).astype(BF).astype(F32)
            z = xz[row_dev:pair, :] * scale
            keep_x[l, s] = x
            conv_sum = pre[s, l] + x * taps[l, taps_count - 1 : taps_count, :]
            for e in range(s):
                tap = taps_count - 1 + e - s
                if tap >= 0:
                    conv_sum = conv_sum + keep_x[l, e] * taps[l, tap : tap + 1, :]
            xc = silu(conv_sum)
            keep_u[l, s] = step_size * xc
            for e in range(s + 1):
                bc = jnp.sum(keep_b[l, e] * c_mat, axis=1, keepdims=True)
                acc_y = keep_d[l, e] * acc_y + keep_u[l, e] * bc
            gated = ((acc_y + head[2, l : l + 1, :] * xc) * silu(z)).astype(BF)
            b_send[k] = gated
            b_recv[k, g] = gated
            for d in range(1, groups):
                peer = lax.rem(g + d, groups)
                cp = remote(b_send.at[k], b_recv.at[k, g], bs_sem.at[d], br_sem.at[k, g], "grp", peer)
                cp.start()
                sends.append(cp)
            for d in range(1, groups):
                src = lax.rem(g + groups - d, groups)
                remote(b_send.at[k], b_recv.at[k, src], bs_sem.at[d], br_sem.at[k, src], "grp", src).wait_recv()
            for i in range(groups):
                gat[i * row_dev : (i + 1) * row_dev, :] = b_recv[k, i].astype(F32)
            gated_all = gat[...].astype(BF)
            if s == 0:
                loads[4 * l + 3].wait()
            for c in range(n_out):
                part = mm(gated_all, wout_v[l, :, c * chunk_out : (c + 1) * chunk_out]).astype(BF)
                c_send[k, c] = part
                c_recv[k, c, t] = part
                for d in range(1, parts):
                    peer = lax.rem(t + d, parts)
                    cp = remote(
                        c_send.at[k, c], c_recv.at[k, c, t], cs_sem.at[c, d], cr_sem.at[k, c, t], "tp", peer
                    )
                    cp.start()
                    sends.append(cp)
            for c in range(n_out):
                for d in range(1, parts):
                    src = lax.rem(t + parts - d, parts)
                    remote(
                        c_send.at[k, c], c_recv.at[k, c, src], cs_sem.at[c, d], cr_sem.at[k, c, src], "tp", src
                    ).wait_recv()
                dsum = c_recv[k, c, 0].astype(F32)
                for i in range(1, parts):
                    dsum = dsum + c_recv[k, c, i].astype(F32)
                cols = slice(c * chunk_out, (c + 1) * chunk_out)
                hxs[:, cols] = (hxs[:, cols] + mm(dup, dsum.astype(BF))).astype(BF).astype(F32)
            for cp in sends:
                cp.wait_send()

        final = mm(undup, hxs[...].astype(BF))
        for _ in range(s):
            final = mm(to_slot, final.astype(BF))
        o32[...] = final
        for i in range(groups):
            o_send[s, i] = o32[i * row_dev : (i + 1) * row_dev, :].astype(BF)

        @pl.when(g // share == t)
        def _(s=s):
            for d in range(1, groups):
                peer = lax.rem(g + d, groups)
                remote(
                    o_send.at[s, peer], o_recv.at[s, lax.rem(g, share)], os_sem.at[s, d],
                    or_sem.at[s, lax.rem(g, share)], "grp", peer,
                ).start()
            o_recv[s, lax.rem(g, share)] = o_send[s, g]

    for s in range(steps):
        for j in range(share):
            src = t * share + j

            @pl.when(src != g)
            def _(s=s, j=j, src=src):
                remote(
                    o_send.at[s, src], o_recv.at[s, j], os_sem.at[s, 1], or_sem.at[s, j], "grp", src
                ).wait_recv()

            out[s, :, j * block : (j + 1) * block] = o_recv[s, j]

    @pl.when(g // share == t)
    def _():
        for s in range(steps):
            for d in range(1, groups):
                peer = lax.rem(g + d, groups)
                remote(
                    o_send.at[s, peer], o_recv.at[s, lax.rem(g, share)], os_sem.at[s, d],
                    or_sem.at[s, lax.rem(g, share)], "grp", peer,
                ).wait_send()


def local(
    embeds, ssm_state, conv_state, norm_gain, in_weight, group_weight, dt_bias, a_log,
    skip_gain, conv_weight, conv_bias, out_weight, leave_row, arrive_from,
):
    groups = lax.axis_size("grp")
    parts = lax.axis_size("tp")
    steps, row_dev, width = embeds.shape
    layers, _, heads_dev, head_dim, state_dim = ssm_state.shape
    block = in_weight.shape[1]
    channels = in_weight.shape[3]
    mix_width = group_weight.shape[2]
    n_heads = mix_width - 2 * state_dim
    rows = groups * row_dev
    pair = 2 * row_dev
    share = groups // parts
    rounds = steps * layers
    chunk_in = min(512, channels)
    chunk_out = min(512, block)
    n_in = channels // chunk_in
    n_out = block // chunk_out

    state = ssm_state.reshape(layers, row_dev, channels, state_dim)
    conv = conv_state.transpose(0, 2, 1, 3)
    w_in = in_weight.reshape(layers, 2 * block, channels)
    head = jnp.repeat(jnp.stack([dt_bias, a_log, skip_gain]), head_dim, axis=2)
    info = jnp.broadcast_to(
        jnp.concatenate([leave_row, arrive_from]).astype(F32)[:, None, None], (2, row_dev, LANES)
    )
    vm = pl.BlockSpec(memory_space=pltpu.VMEM)
    anywhere = pl.BlockSpec(memory_space=pl.ANY)
    dma = pltpu.SemaphoreType.DMA
    V = pltpu.VMEM
    return pl.pallas_call(
        functools.partial(kernel, groups, parts, heads_dev, head_dim, chunk_in, chunk_out),
        out_shape=jax.ShapeDtypeStruct((steps, row_dev, width // parts), BF),
        in_specs=[vm] * 7 + [anywhere] * 4,
        out_specs=vm,
        scratch_shapes=[
            V((layers, 2 * block, channels), BF),
            V((layers, block, mix_width), BF),
            V((layers, channels, block), BF),
            V((layers, row_dev, channels, state_dim), BF),
            V((groups, steps, row_dev, block), BF),
            V((groups, 2, row_dev, LANES), F32),
            V((steps, rows, block), F32),
            V((2, rows, LANES), F32),
            V((steps, layers, row_dev, channels), F32),
            V((n_heads, channels), BF),
            V((2 * rows, 2 * block), BF),
            V((2 * rows, block), F32),
            V((groups, row_dev, mix_width + LANES), F32),
            V((rounds, groups, row_dev, mix_width + LANES), F32),
            V((n_in, groups, pair, chunk_in), BF),
            V((rounds, n_in, groups, pair, chunk_in), BF),
            V((rounds, row_dev, channels), BF),
            V((rounds, groups, row_dev, channels), BF),
            V((rounds, n_out, rows, chunk_out), BF),
            V((rounds, n_out, parts, rows, chunk_out), BF),
            V((steps, groups, row_dev, block), BF),
            V((steps, share, row_dev, block), BF),
            V((pair, state_dim), F32),
            V((pair, channels), F32),
            V((pair, channels), F32),
            V((rows, channels), F32),
            V((rows, block), F32),
            V((layers, steps, row_dev, channels), F32),
            V((layers, steps, row_dev, channels), F32),
            V((layers, steps, row_dev, channels), F32),
            V((layers, steps, row_dev, state_dim), F32),
            dma((layers, 4)),
            dma((groups,)),
            dma((groups,)),
            dma((groups,)),
            dma((groups,)),
            dma((groups,)),
            dma((rounds, groups)),
            dma((n_in, groups)),
            dma((rounds, n_in, groups)),
            dma((groups,)),
            dma((rounds, groups)),
            dma((n_out, parts)),
            dma((rounds, n_out, parts)),
            dma((steps, groups)),
            dma((steps, share)),
        ],
        compiler_params=pltpu.CompilerParams(
            collective_id=0, has_side_effects=True, vmem_limit_bytes=60 * 2**20
        ),
    )(embeds, conv, norm_gain, head, conv_weight, conv_bias, info, state, w_in, group_weight, out_weight)


def solution(mesh):
    placed = (
        P(None, "grp", None),
        P(None, "grp", "tp", None, None),
        P(None, "grp", None, "tp"),
        P(),
        P(None, "grp", None, "tp"),
        P(None, "grp", None),
        P(None, "tp"),
        P(None, "tp"),
        P(None, "tp"),
        P(None, None, "tp"),
        P(None, "tp"),
        P(None, "tp", "grp"),
        P("grp"),
        P("grp"),
    )
    return jax.shard_map(
        local, mesh=mesh, in_specs=placed, out_specs=P(None, "grp", "tp"), check_vma=False
    )
```

```python
import functools

import jax
import jax.numpy as jnp
from jax import lax
from jax.experimental import pallas as pl
from jax.experimental.pallas import tpu as pltpu
from jax.sharding import PartitionSpec as P

F32 = jnp.float32
BF = jnp.bfloat16
LANES = 128


def iota(shape, dim):
    return lax.broadcasted_iota(jnp.int32, shape, dim)


def mm(a, b):
    return jnp.dot(a, b, preferred_element_type=F32)


def silu(v):
    return v / (1.0 + jnp.exp(-v))


def remote(src, dst, send_sem, recv_sem, axis, peer):
    return pltpu.make_async_remote_copy(
        src_ref=src,
        dst_ref=dst,
        send_sem=send_sem,
        recv_sem=recv_sem,
        device_id={axis: peer},
        device_id_type=pl.DeviceIdType.MESH,
    )


def kernel(
    groups, parts, heads_dev, head_dim, chunk_in, chunk_out,
    emb, conv, gain, dt_bias, a_log, skip, taps, cbias, leave, arrive, state, w_in, w_grp, w_out,
    out,
    win_v, wg_v, wout_v, st_v,
    emb_r, info_r, e32, info32, pre, sel, lhs, hxs,
    head, info, m_send, m_pair, m_z, m_recv, a_send, a_pair, a_z, a_recv, b_send, b_recv, c_send, c_recv, o_send, o_recv,
    hl, y8, xz, gat, o32, keep_d, keep_u, keep_x, keep_b,
    load_sem, in_sem, es_sem, er_sem, is_sem, ir_sem, mps_sem, mpr_sem, ms_sem, mr_sem,
    aps_sem, apr_sem, as_sem, ar_sem,
    bs_sem, br_sem, cs_sem, cr_sem, os_sem, or_sem,
):
    g = lax.axis_index("grp")
    t = lax.axis_index("tp")
    steps, row_dev, width = emb.shape
    layers = gain.shape[0]
    block = width // groups
    rows = groups * row_dev
    pair = 2 * row_dev
    channels = taps.shape[2]
    taps_count = taps.shape[1]
    state_dim = st_v.shape[3]
    mix_width = wg_v.shape[2]
    n_in = channels // chunk_in
    n_out = block // chunk_out
    share = groups // parts
    half = groups // 2
    core = lax.rem(g, 2)
    chip = g // 2
    partner = g + 1 - 2 * core
    n_tiles = channels // LANES
    tiles_in = chunk_in // LANES

    loads = {}
    for l in range(layers):
        plan = [("grp", w_grp.at[l], wg_v.at[l], load_sem.at[l, 0])]
        for n in range(n_tiles):
            tile = slice(n * LANES, (n + 1) * LANES)
            plan.append((n, w_in.at[l, :, :, tile], win_v.at[l, n], in_sem.at[l, n]))
        plan.append(("state", state.at[l], st_v.at[l], load_sem.at[l, 1]))
        plan.append(("out", w_out.at[l], wout_v.at[l], load_sem.at[l, 2]))
        for name, src, dst, sem in plan:
            loads[l, name] = pltpu.make_async_copy(src, dst, sem)
            loads[l, name].start()
    info[0] = jnp.full((row_dev, LANES), leave[0].astype(F32), F32)
    info[1] = jnp.full((row_dev, LANES), arrive[0].astype(F32), F32)

    barrier = pltpu.get_barrier_semaphore()
    for d in range(1, groups):
        pl.semaphore_signal(
            barrier, inc=1, device_id={"grp": lax.rem(g + d, groups)},
            device_id_type=pl.DeviceIdType.MESH,
        )
    for d in range(1, parts):
        pl.semaphore_signal(
            barrier, inc=1, device_id={"tp": lax.rem(t + d, parts)},
            device_id_type=pl.DeviceIdType.MESH,
        )
    pl.semaphore_wait(barrier, groups - 1 + parts - 1)

    def columns(who):
        return pl.ds(pl.multiple_of(who * block, block), block)

    first_sends = []
    for d in range(1, groups):
        peer = lax.rem(g + d, groups)
        cp = remote(emb.at[:, :, columns(peer)], emb_r.at[g], es_sem.at[d], er_sem.at[g], "grp", peer)
        cp.start()
        first_sends.append(cp)
        cp = remote(info, info_r.at[g], is_sem.at[d], ir_sem.at[g], "grp", peer)
        cp.start()
        first_sends.append(cp)
    emb_r[g] = emb[:, :, columns(g)]
    info_r[g] = info[...]

    for s in range(steps):
        for l in range(layers):
            total = jnp.zeros((row_dev, channels), F32)
            for k in range(taps_count - 1):
                if s + k <= taps_count - 2:
                    total = total + conv[l, s + k].astype(F32) * taps[l, k : k + 1, :]
            pre[s, l] = total + cbias[l : l + 1, :]
    n_heads = sel.shape[0]
    sel[...] = (
        iota((n_heads, channels), 0) == t * heads_dev + iota((n_heads, channels), 1) // head_dim
    ).astype(F32).astype(BF)
    own_head = (
        iota((heads_dev, channels), 1) // head_dim == iota((heads_dev, channels), 0)
    ).astype(F32).astype(BF)
    for i, param in enumerate((dt_bias, a_log, skip)):
        rest = param[...]
        wide = jnp.zeros((layers, channels), F32)
        for _ in range(3):
            piece = rest.astype(BF)
            rest = rest - piece.astype(F32)
            wide = wide + mm(piece, own_head)
        head[i] = wide
    dup_row = iota((2 * rows, rows), 0)
    dup = (
        iota((2 * rows, rows), 1) == (dup_row // pair) * row_dev + lax.rem(dup_row, row_dev)
    ).astype(F32).astype(BF)
    und_col = iota((rows, 2 * rows), 1)
    und_row = iota((rows, 2 * rows), 0)
    undup = (
        und_col == (und_row // row_dev) * pair + lax.rem(und_row, row_dev)
    ).astype(F32).astype(BF)
    spread = (
        iota((LANES, 2 * LANES), 1) // 2 == iota((LANES, 2 * LANES), 0)
    ).astype(F32).astype(BF)
    own_half = lax.rem(iota((2 * rows, 2 * LANES), 1), 2) == lax.rem(
        iota((2 * rows, 2 * LANES), 0) // row_dev, 2
    )

    for d in range(1, groups):
        src = lax.rem(g + groups - d, groups)
        remote(emb.at[:, :, columns(src)], emb_r.at[src], es_sem.at[d], er_sem.at[src], "grp", src).wait_recv()
        remote(info, info_r.at[src], is_sem.at[d], ir_sem.at[src], "grp", src).wait_recv()
    for i in range(groups):
        for s in range(steps):
            e32[s, i * row_dev : (i + 1) * row_dev, :] = emb_r[i, s].astype(F32)
        for q in range(2):
            info32[q, i * row_dev : (i + 1) * row_dev, :] = info_r[i, q]

    row_i = iota((rows, LANES), 0)
    col_i = iota((rows, LANES), 1)
    on_diag = row_i == col_i
    leave_of_row = info32[0]
    from_of_row = info32[1]
    leave_of_col = jnp.sum(jnp.where(on_diag, leave_of_row, 0.0), axis=0, keepdims=True)
    from_of_col = jnp.sum(jnp.where(on_diag, from_of_row, 0.0), axis=0, keepdims=True)
    slot_row = lax.rem(row_i, row_dev).astype(F32)
    slot_col = lax.rem(col_i, row_dev).astype(F32)
    group_row = (row_i // row_dev).astype(F32)
    group_col = (col_i // row_dev).astype(F32)
    diag = jnp.where(on_diag, 1.0, 0.0)
    hit = jnp.where(group_col == from_of_row, 1.0, 0.0) * jnp.where(slot_col == leave_of_col, 1.0, 0.0)
    to_slot = jnp.where(slot_row == leave_of_row, hit, diag)[:, :rows].astype(BF)
    hit_t = jnp.where(group_row == from_of_col, 1.0, 0.0) * jnp.where(slot_row == leave_of_row, 1.0, 0.0)
    to_home = jnp.where(slot_col == leave_of_col, hit_t, diag)[:, :rows].astype(BF)

    for cp in first_sends:
        cp.wait_send()

    out_sends = []
    for s in range(steps):
        start = e32[s].astype(BF)
        for _ in range(s):
            start = mm(to_home, start).astype(BF)
        hxs[...] = mm(dup, start)
        for l in range(layers):
            k = s * layers + l
            sends = []
            hx = hxs[...]
            gained = (hx * gain[l : l + 1, columns(g)]).astype(BF)
            if s == 0:
                loads[l, "grp"].wait()
            mix = mm(gained, wg_v[l])
            square = jnp.broadcast_to(jnp.sum(hx * hx, axis=1, keepdims=True), (2 * rows, LANES))
            for i in range(groups):
                m_send[i % 2, i // 2, :, :mix_width] = mix[i * pair : i * pair + row_dev]
                m_send[i % 2, i // 2, :, mix_width:] = square[i * pair : i * pair + row_dev]
            m_cross = remote(m_send.at[1 - core], m_pair.at[k], mps_sem.at[0], mpr_sem.at[k], "grp", partner)
            m_cross.start()
            sends.append(m_cross)
            for j in range(block // LANES):
                wide = mm(gained[:, j * LANES : (j + 1) * LANES], spread)
                lhs[:, 2 * j * LANES : 2 * (j + 1) * LANES] = jnp.where(own_half, wide, 0.0).astype(BF)
            crossing = []
            for c in range(n_in + 1):
                if c < n_in:
                    tiles = []
                    for n in range(c * tiles_in, (c + 1) * tiles_in):
                        if s == 0:
                            loads[l, n].wait()
                        tiles.append(win_v[l, n].reshape(2 * block, LANES))
                    acc = mm(lhs[...], jnp.concatenate(tiles, axis=1))
                    for i in range(groups):
                        a_send[c, i % 2, i // 2] = acc[i * pair : (i + 1) * pair].astype(BF)
                    cross = remote(
                        a_send.at[c, 1 - core], a_pair.at[k, c], aps_sem.at[c], apr_sem.at[k, c], "grp", partner
                    )
                    cross.start()
                    sends.append(cross)
                    crossing.append(cross)
                if c == 0:
                    m_cross.wait_recv()
                    m_z[...] = m_send[core] + m_pair[k]
                    for d in range(1, half):
                        to = lax.rem(chip + d, half)
                        cp = remote(
                            m_z.at[to], m_recv.at[k, chip], ms_sem.at[d], mr_sem.at[k, chip], "grp", 2 * to + core
                        )
                        cp.start()
                        sends.append(cp)
                    m_recv[k, chip] = m_z[chip]
                else:
                    e = c - 1
                    crossing[e].wait_recv()
                    a_z[e] = (a_send[e, core].astype(F32) + a_pair[k, e].astype(F32)).astype(BF)
                    for d in range(1, half):
                        to = lax.rem(chip + d, half)
                        cp = remote(
                            a_z.at[e, to], a_recv.at[k, e, chip], as_sem.at[e, d], ar_sem.at[k, e, chip],
                            "grp", 2 * to + core,
                        )
                        cp.start()
                        sends.append(cp)
                    a_recv[k, e, chip] = a_z[e, chip]

            for d in range(1, half):
                src = lax.rem(chip + half - d, half)
                remote(
                    m_z.at[src], m_recv.at[k, src], ms_sem.at[d], mr_sem.at[k, src], "grp", 2 * src + core
                ).wait_recv()
            msum = m_recv[k, 0]
            for i in range(1, half):
                msum = msum + m_recv[k, i]
            scale = lax.rsqrt(msum[:, mix_width : mix_width + 1] / width + 1e-05)
            b_mat = msum[:, :state_dim] * scale
            c_mat = msum[:, state_dim : 2 * state_dim] * scale
            dt_all = msum[:, 2 * state_dim : mix_width] * scale
            keep_b[l, s] = b_mat
            dt_hi = dt_all.astype(BF)
            dt_lo = (dt_all - dt_hi.astype(F32)).astype(BF)
            dt_ch = mm(dt_hi, sel[...]) + mm(dt_lo, sel[...])
            pre_dt = dt_ch + head[0, l : l + 1, :]
            step_size = jnp.maximum(pre_dt, 0.0) + jnp.log1p(jnp.exp(-jnp.abs(pre_dt)))
            keep_d[l, s] = jnp.exp(-step_size * jnp.exp(head[1, l : l + 1, :]))
            c_hi = c_mat.astype(BF).astype(F32)
            hl[0:row_dev, :] = c_hi
            hl[row_dev:pair, :] = c_mat - c_hi
            c_both = hl[...].astype(BF)
            if s == 0:
                loads[l, "state"].wait()
            slot8 = lax.rem(iota((pair, channels), 0), row_dev)
            total = jnp.zeros((pair, channels), F32)
            for r in range(row_dev):
                got = lax.dot_general(
                    c_both, st_v[l, r], (((1,), (1,)), ((), ())), preferred_element_type=F32
                )
                total = jnp.where(slot8 == r, got, total)
            y8[...] = total
            acc_y = y8[0:row_dev, :] + y8[row_dev:pair, :]

            for c in range(n_in):
                for d in range(1, half):
                    src = lax.rem(chip + half - d, half)
                    remote(
                        a_z.at[c, src], a_recv.at[k, c, src], as_sem.at[c, d], ar_sem.at[k, c, src],
                        "grp", 2 * src + core,
                    ).wait_recv()
                asum = a_recv[k, c, 0].astype(F32)
                for i in range(1, half):
                    asum = asum + a_recv[k, c, i].astype(F32)
                xz[:, c * chunk_in : (c + 1) * chunk_in] = asum
            x = (xz[0:row_dev, :] * scale).astype(BF).astype(F32)
            z = xz[row_dev:pair, :] * scale
            keep_x[l, s] = x
            conv_sum = pre[s, l] + x * taps[l, taps_count - 1 : taps_count, :]
            for e in range(s):
                tap = taps_count - 1 + e - s
                if tap >= 0:
                    conv_sum = conv_sum + keep_x[l, e] * taps[l, tap : tap + 1, :]
            xc = silu(conv_sum)
            keep_u[l, s] = step_size * xc
            for e in range(s + 1):
                bc = jnp.sum(keep_b[l, e] * c_mat, axis=1, keepdims=True)
                acc_y = keep_d[l, e] * acc_y + keep_u[l, e] * bc
            gated = ((acc_y + head[2, l : l + 1, :] * xc) * silu(z)).astype(BF)
            b_send[k] = gated
            b_recv[k, g] = gated
            for d in range(1, groups):
                peer = lax.rem(g + d, groups)
                cp = remote(b_send.at[k], b_recv.at[k, g], bs_sem.at[d], br_sem.at[k, g], "grp", peer)
                cp.start()
                sends.append(cp)
            for d in range(1, groups):
                src = lax.rem(g + groups - d, groups)
                remote(b_send.at[k], b_recv.at[k, src], bs_sem.at[d], br_sem.at[k, src], "grp", src).wait_recv()
            for i in range(groups):
                gat[i * row_dev : (i + 1) * row_dev, :] = b_recv[k, i].astype(F32)
            gated_all = gat[...].astype(BF)
            if s == 0:
                loads[l, "out"].wait()
            for c in range(n_out):
                part = mm(gated_all, wout_v[l, :, c * chunk_out : (c + 1) * chunk_out]).astype(BF)
                c_send[k, c] = part
                c_recv[k, c, t] = part
                for d in range(1, parts):
                    peer = lax.rem(t + d, parts)
                    cp = remote(
                        c_send.at[k, c], c_recv.at[k, c, t], cs_sem.at[c, d], cr_sem.at[k, c, t], "tp", peer
                    )
                    cp.start()
                    sends.append(cp)
            for c in range(n_out):
                for d in range(1, parts):
                    src = lax.rem(t + parts - d, parts)
                    remote(
                        c_send.at[k, c], c_recv.at[k, c, src], cs_sem.at[c, d], cr_sem.at[k, c, src], "tp", src
                    ).wait_recv()
                dsum = c_recv[k, c, 0].astype(F32)
                for i in range(1, parts):
                    dsum = dsum + c_recv[k, c, i].astype(F32)
                cols = slice(c * chunk_out, (c + 1) * chunk_out)
                hxs[:, cols] = (hxs[:, cols] + mm(dup, dsum.astype(BF))).astype(BF).astype(F32)
            for cp in sends:
                cp.wait_send()

        final = mm(undup, hxs[...].astype(BF))
        for _ in range(s):
            final = mm(to_slot, final.astype(BF))
        o32[...] = final
        for i in range(groups):
            o_send[s, i] = o32[i * row_dev : (i + 1) * row_dev, :].astype(BF)

        @pl.when(g // share == t)
        def _(s=s):
            for d in range(1, groups):
                peer = lax.rem(g + d, groups)
                remote(
                    o_send.at[s, peer], o_recv.at[s, lax.rem(g, share)], os_sem.at[s, d],
                    or_sem.at[s, lax.rem(g, share)], "grp", peer,
                ).start()
            o_recv[s, lax.rem(g, share)] = o_send[s, g]

    for s in range(steps):
        for j in range(share):
            src = t * share + j

            @pl.when(src != g)
            def _(s=s, j=j, src=src):
                remote(
                    o_send.at[s, src], o_recv.at[s, j], os_sem.at[s, 1], or_sem.at[s, j], "grp", src
                ).wait_recv()

            out[s, :, j * block : (j + 1) * block] = o_recv[s, j]

    @pl.when(g // share == t)
    def _():
        for s in range(steps):
            for d in range(1, groups):
                peer = lax.rem(g + d, groups)
                remote(
                    o_send.at[s, peer], o_recv.at[s, lax.rem(g, share)], os_sem.at[s, d],
                    or_sem.at[s, lax.rem(g, share)], "grp", peer,
                ).wait_send()


def local(
    embeds, ssm_state, conv_state, norm_gain, in_weight, group_weight, dt_bias, a_log,
    skip_gain, conv_weight, conv_bias, out_weight, leave_row, arrive_from,
):
    groups = lax.axis_size("grp")
    parts = lax.axis_size("tp")
    steps, row_dev, width = embeds.shape
    layers, _, heads_dev, head_dim, state_dim = ssm_state.shape
    block = in_weight.shape[1]
    channels = in_weight.shape[3]
    mix_width = group_weight.shape[2]
    n_heads = mix_width - 2 * state_dim
    rows = groups * row_dev
    pair = 2 * row_dev
    share = groups // parts
    half = groups // 2
    rounds = steps * layers
    chunk_in = min(512, channels)
    chunk_out = min(512, block)
    n_in = channels // chunk_in
    n_out = block // chunk_out

    state = ssm_state.reshape(layers, row_dev, channels, state_dim)
    conv = conv_state.transpose(0, 2, 1, 3)
    vm = pl.BlockSpec(memory_space=pltpu.VMEM)
    anywhere = pl.BlockSpec(memory_space=pl.ANY)
    dma = pltpu.SemaphoreType.DMA
    V = pltpu.VMEM
    return pl.pallas_call(
        functools.partial(kernel, groups, parts, heads_dev, head_dim, chunk_in, chunk_out),
        out_shape=jax.ShapeDtypeStruct((steps, row_dev, width // parts), BF),
        in_specs=[vm] * 8 + [pl.BlockSpec(memory_space=pltpu.SMEM)] * 2 + [anywhere] * 4,
        out_specs=vm,
        scratch_shapes=[
            V((layers, channels // LANES, block, 2, LANES), BF),
            V((layers, block, mix_width), BF),
            V((layers, channels, block), BF),
            V((layers, row_dev, channels, state_dim), BF),
            V((groups, steps, row_dev, block), BF),
            V((groups, 2, row_dev, LANES), F32),
            V((steps, rows, block), F32),
            V((2, rows, LANES), F32),
            V((steps, layers, row_dev, channels), F32),
            V((n_heads, channels), BF),
            V((2 * rows, 2 * block), BF),
            V((2 * rows, block), F32),
            V((3, layers, channels), F32),
            V((2, row_dev, LANES), F32),
            V((2, half, row_dev, mix_width + LANES), F32),
            V((rounds, half, row_dev, mix_width + LANES), F32),
            V((half, row_dev, mix_width + LANES), F32),
            V((rounds, half, row_dev, mix_width + LANES), F32),
            V((n_in, 2, half, pair, chunk_in), BF),
            V((rounds, n_in, half, pair, chunk_in), BF),
            V((n_in, half, pair, chunk_in), BF),
            V((rounds, n_in, half, pair, chunk_in), BF),
            V((rounds, row_dev, channels), BF),
            V((rounds, groups, row_dev, channels), BF),
            V((rounds, n_out, rows, chunk_out), BF),
            V((rounds, n_out, parts, rows, chunk_out), BF),
            V((steps, groups, row_dev, block), BF),
            V((steps, share, row_dev, block), BF),
            V((pair, state_dim), F32),
            V((pair, channels), F32),
            V((pair, channels), F32),
            V((rows, channels), F32),
            V((rows, block), F32),
            V((layers, steps, row_dev, channels), F32),
            V((layers, steps, row_dev, channels), F32),
            V((layers, steps, row_dev, channels), F32),
            V((layers, steps, row_dev, state_dim), F32),
            dma((layers, 3)),
            dma((layers, channels // LANES)),
            dma((groups,)),
            dma((groups,)),
            dma((groups,)),
            dma((groups,)),
            dma((1,)),
            dma((rounds,)),
            dma((half,)),
            dma((rounds, half)),
            dma((n_in,)),
            dma((rounds, n_in)),
            dma((n_in, half)),
            dma((rounds, n_in, half)),
            dma((groups,)),
            dma((rounds, groups)),
            dma((n_out, parts)),
            dma((rounds, n_out, parts)),
            dma((steps, groups)),
            dma((steps, share)),
        ],
        compiler_params=pltpu.CompilerParams(
            collective_id=0, has_side_effects=True, vmem_limit_bytes=60 * 2**20
        ),
    )(
        embeds, conv, norm_gain, dt_bias, a_log, skip_gain, conv_weight, conv_bias, leave_row, arrive_from,
        state, in_weight, group_weight, out_weight,
    )


def solution(mesh):
    placed = (
        P(None, "grp", None),
        P(None, "grp", "tp", None, None),
        P(None, "grp", None, "tp"),
        P(),
        P(None, "grp", None, "tp"),
        P(None, "grp", None),
        P(None, "tp"),
        P(None, "tp"),
        P(None, "tp"),
        P(None, None, "tp"),
        P(None, "tp"),
        P(None, "tp", "grp"),
        P("grp"),
        P("grp"),
    )
    return jax.shard_map(
        local, mesh=mesh, in_specs=placed, out_specs=P(None, "grp", "tp"), check_vma=False
    )
```
